128 devices in a mesh: state: 2 (over x_lo), mode: 64 (over y, x_hi, z, core).
Axes of the slice: x: 4 (x_hi: 2, x_lo: 2; x = x_hi * 2 + x_lo), y: 4, z: 4, core: 2. Of those that a mesh axis runs over, the one named last changes fastest.
Arguments:
- core: bfloat16 [2, 512, 512, 256], P('state', 'mode'), may hold values from -6 to 6
- op_one: bfloat16 [2, 3, 512, 512], replicated, may hold values from -0.25 to 0.25
- op_two: bfloat16 [2, 3, 512, 512], replicated, may hold values from -0.25 to 0.25
- op_three: bfloat16 [2, 3, 256, 256], replicated, may hold values from -0.375 to 0.375
Outputs:
- relaxed: float32 [2, 512, 512, 256], P('state', 'mode')
The draws below stay inside these ranges and needn't reach their ends.
All inputs are finite; a program needn't handle non-finite values.
Results may differ from the reference program's by a relative error of at most 0.0033.
Values may be sent and summed in bfloat16 or wider, within the bound.
No kernel may reach another device: no remote copies, remote signals or barrier semaphores. Data moves between devices by JAX's collectives and lax.ppermute only.
A program may use at most 64 MiB of HBM per device.

```python
import jax
import jax.numpy as jnp
from jax import lax

N1 = 512
N2 = 512
N3 = 256
TERMS = 3
N_STATE = 2


def shard_levels(rng, extent, shards, least, top_value):
    gain, own = 1.0, jax.random.fold_in(rng, 6)
    for dim, shards_of in shards:
        heights = jnp.exp(jax.random.uniform(jax.random.fold_in(own, dim), (shards_of,), jnp.float32, least / len(shards), top_value / len(shards)))
        gain = gain * jnp.repeat(heights, extent[dim] // shards_of).reshape([-1 if axis == dim else 1 for axis in range(len(extent))])
    return gain


def gaussian(stream_key, shape, deviation, limit, shards=(), held_as=jnp.bfloat16):
    entries = jax.random.normal(stream_key, shape, jnp.float32) * deviation
    if len(shards) > 0:
        entries = shard_levels(stream_key, shape, shards, -0.22, 0.18) * entries
    return jnp.clip(entries, min=-limit, max=limit).astype(held_as)


def setup_inputs(seed: int = 0) -> dict:
    arg_keys = jax.random.split(jax.random.key(seed), 5)
    return {
        "core": gaussian(arg_keys[0], (N_STATE, N1, N2, N3), 1.0, 6.0, ((0, 2), (1, 64))),
        "op_one": gaussian(arg_keys[1], (N_STATE, TERMS, N1, N1), N1 ** -0.5, 0.25),
        "op_two": gaussian(arg_keys[2], (N_STATE, TERMS, N2, N2), N2 ** -0.5, 0.25),
        "op_three": gaussian(arg_keys[3], (N_STATE, TERMS, N3, N3), N3 ** -0.5, 0.375),
    }


def apply_term(block, first, second, third):
    inner = jnp.einsum("ijk,lk->ijl", block.astype(jnp.float32), third.astype(jnp.float32)).astype(jnp.bfloat16)
    inner = lax.optimization_barrier(inner)
    prepared = jnp.einsum("ab,ibk->iak", second.astype(jnp.float32), inner.astype(jnp.float32)).astype(jnp.bfloat16)
    prepared = lax.optimization_barrier(prepared)
    return jnp.einsum("ab,bjk->ajk", first.astype(jnp.float32), prepared.astype(jnp.float32))


def reference(core, op_one, op_two, op_three):
    diagonal_parts = []
    coupling_parts = []
    for state_number in range(N_STATE):
        block = core[state_number]
        diagonal_value = apply_term(block, op_one[state_number, 0], op_two[state_number, 0], op_three[state_number, 0])
        diagonal_value = diagonal_value + apply_term(block, op_one[state_number, 1], op_two[state_number, 1], op_three[state_number, 1])
        diagonal_parts.append(diagonal_value)
        coupling_parts.append(apply_term(block, op_one[state_number, 2], op_two[state_number, 2], op_three[state_number, 2]))
    results = []
    for state_number in range(N_STATE):
        combined = diagonal_parts[state_number] + coupling_parts[1 - state_number]
        applied = lax.optimization_barrier(combined.astype(jnp.bfloat16))
        results.append(core[state_number].astype(jnp.float32) - 0.5 * applied.astype(jnp.float32))
    return jnp.stack(results)
```

```python
import jax
import jax.numpy as jnp
from jax import lax
from jax.sharding import PartitionSpec as P

EVERY = ("state", "mode")


def shards(core, op_one, op_two, op_three):
    own_core = core[0]
    rows, second_extent, third_extent = own_core.shape
    states, terms, first_extent, _ = op_one.shape
    owners = first_extent // rows
    columns = second_extent // (states * owners)
    state_index = lax.axis_index("state")
    own_second = lax.dynamic_index_in_dim(op_two, state_index, 0, keepdims=False)
    own_third = lax.dynamic_index_in_dim(op_three, state_index, 0, keepdims=False)
    prepared = []
    for term in range(terms):
        inner = jnp.einsum(
            "ijk,lk->jil", own_core, own_third[term], preferred_element_type=jnp.float32
        ).astype(jnp.bfloat16)
        prepared.append(
            jnp.einsum(
                "ab,bik->aik", own_second[term], inner, preferred_element_type=jnp.float32
            ).astype(jnp.bfloat16)
        )
    pieces = [
        lax.all_to_all(value, EVERY, split_axis=0, concat_axis=0, tiled=True).reshape(
            states, owners, columns, rows, third_extent
        )
        for value in prepared
    ]
    pieces = [
        value.transpose(0, 1, 3, 2, 4).reshape(states, first_extent, columns, third_extent)
        for value in pieces
    ]
    applied = []
    for state in range(states):
        sources = [(state, 0), (state, 1), (1 - state, 2)]
        total = sum(
            jnp.einsum(
                "ab,bjk->ajk",
                op_one[source, term],
                pieces[term][source],
                preferred_element_type=jnp.float32,
            )
            for source, term in sources
        )
        applied.append(total.astype(jnp.bfloat16))
    sent = jnp.stack(applied).reshape(states, owners, rows, columns, third_extent)
    sent = sent.transpose(0, 1, 3, 2, 4).reshape(second_extent, rows, third_extent)
    returned = lax.all_to_all(sent, EVERY, split_axis=0, concat_axis=0, tiled=True)
    returned = returned.reshape(second_extent, rows, third_extent)
    relaxed = own_core.astype(jnp.float32) - 0.5 * returned.transpose(1, 0, 2).astype(jnp.float32)
    return relaxed[None]


def solution(mesh):
    placed = (P("state", "mode", None, None), P(), P(), P())
    return jax.shard_map(
        shards,
        mesh=mesh,
        in_specs=placed,
        out_specs=P("state", "mode", None, None),
        check_vma=False,
    )
```

```python
import jax
import jax.numpy as jnp
from jax import lax
from jax.experimental import pallas as pl
from jax.experimental.pallas import tpu as pltpu
from jax.sharding import PartitionSpec as P

EVERY = ("state", "mode")
LANES = 128


def prepare(state_ref, core_ref, second_ref, third_ref, sent_ref, rows_ref):
    rows, second_extent, third_extent = core_ref.shape
    second = second_ref[0, 0]
    third = third_ref[0, 0]

    def one_row(row, carry):
        inner = lax.dot_general(
            core_ref[row],
            third,
            (((1,), (1,)), ((), ())),
            preferred_element_type=jnp.float32,
        ).astype(jnp.bfloat16)
        value = jnp.dot(second, inner, preferred_element_type=jnp.float32)
        for part in range(third_extent // LANES):
            rows_ref[part, pl.ds(row, second_extent, stride=rows), :] = value[
                :, part * LANES : (part + 1) * LANES
            ]
        return carry

    lax.fori_loop(0, rows, one_row, 0)
    for part in range(third_extent // LANES):
        sent_ref[:, 0, :, part * LANES : (part + 1) * LANES] = (
            rows_ref[part].astype(jnp.bfloat16).reshape(*sent_ref.shape[:1], sent_ref.shape[2], LANES)
        )


def apply_first(first_ref, got_ref, sent_ref):
    states, _, first_extent, _ = first_ref.shape
    devices, terms, held, third_extent = got_ref.shape
    owners = devices // states
    rows = first_extent // owners

    def piece(source, term, column):
        value = got_ref[
            source * owners : (source + 1) * owners, term, column * rows : (column + 1) * rows
        ]
        return (
            value.astype(jnp.float32).reshape(first_extent, third_extent).astype(jnp.bfloat16)
        )

    for column in range(held // rows):
        for state in range(states):
            total = jnp.zeros((first_extent, third_extent), jnp.float32)
            for source, term in ((state, 0), (state, 1), (1 - state, 2)):
                total += jnp.dot(
                    first_ref[source, term],
                    piece(source, term, column),
                    preferred_element_type=jnp.float32,
                )
            sent_ref[
                state * owners : (state + 1) * owners, column * rows : (column + 1) * rows
            ] = total.reshape(owners, rows, third_extent).astype(jnp.bfloat16)


def relax(got_ref, core_ref, relaxed_ref, rows_ref):
    row = pl.program_id(0)
    rows = pl.num_programs(0)

    @pl.when(row == 0)
    def _():
        for part in range(rows_ref.shape[0]):
            rows_ref[part] = (
                got_ref[:, :, part * LANES : (part + 1) * LANES]
                .astype(jnp.float32)
                .reshape(rows_ref.shape[1:])
            )

    for part in range(rows_ref.shape[0]):
        lanes = slice(part * LANES, (part + 1) * LANES)
        applied = rows_ref[part, pl.ds(row, core_ref.shape[1], stride=rows), :]
        relaxed_ref[0, :, lanes] = core_ref[0, :, lanes].astype(jnp.float32) - 0.5 * applied


def shards(core, op_one, op_two, op_three):
    own_core = core[0]
    rows, second_extent, third_extent = own_core.shape
    states, terms, first_extent, _ = op_one.shape
    devices = states * (first_extent // rows)
    held = second_extent // devices * rows
    state_index = lax.axis_index("state").astype(jnp.int32).reshape(1)
    whole = pl.BlockSpec(memory_space=pltpu.VMEM)

    sent = pl.pallas_call(
        prepare,
        grid_spec=pltpu.PrefetchScalarGridSpec(
            num_scalar_prefetch=1,
            grid=(terms,),
            in_specs=[
                pl.BlockSpec((rows, second_extent, third_extent), lambda term, state: (0, 0, 0)),
                pl.BlockSpec(
                    (1, 1, second_extent, second_extent), lambda term, state: (state[0], term, 0, 0)
                ),
                pl.BlockSpec(
                    (1, 1, third_extent, third_extent), lambda term, state: (state[0], term, 0, 0)
                ),
            ],
            out_specs=pl.BlockSpec(
                (devices, 1, held, third_extent), lambda term, state: (0, term, 0, 0)
            ),
            scratch_shapes=[pltpu.VMEM((third_extent // LANES, rows * second_extent, LANES), jnp.float32)],
        ),
        out_shape=jax.ShapeDtypeStruct((devices, terms, held, third_extent), jnp.bfloat16),
        name="prepare",
    )(state_index, own_core, op_two, op_three)
    got = lax.all_to_all(sent, EVERY, split_axis=0, concat_axis=0, tiled=True)
    applied = pl.pallas_call(
        apply_first,
        in_specs=[whole, whole],
        out_specs=whole,
        out_shape=jax.ShapeDtypeStruct((devices, held, third_extent), jnp.bfloat16),
        name="apply_first",
    )(op_one, got)
    returned = lax.all_to_all(applied, EVERY, split_axis=0, concat_axis=0, tiled=True)
    relaxed = pl.pallas_call(
        relax,
        grid=(rows,),
        in_specs=[
            pl.BlockSpec((devices, held, third_extent), lambda row: (0, 0, 0)),
            pl.BlockSpec((1, second_extent, third_extent), lambda row: (row, 0, 0)),
        ],
        out_specs=pl.BlockSpec((1, second_extent, third_extent), lambda row: (row, 0, 0)),
        scratch_shapes=[pltpu.VMEM((third_extent // LANES, rows * second_extent, LANES), jnp.float32)],
        out_shape=jax.ShapeDtypeStruct(own_core.shape, jnp.float32),
        name="relax",
    )(returned, own_core)
    return relaxed[None]


def solution(mesh):
    placed = (P("state", "mode", None, None), P(), P(), P())
    return jax.shard_map(
        shards,
        mesh=mesh,
        in_specs=placed,
        out_specs=P("state", "mode", None, None),
        check_vma=False,
    )
```

```python
import jax
import jax.numpy as jnp
from jax import lax
from jax.experimental import pallas as pl
from jax.experimental.pallas import tpu as pltpu
from jax.sharding import PartitionSpec as P

EVERY = ("state", "mode")
LANES = 128
UNROLL = 8


def prepare(state_ref, core_ref, second_ref, third_ref, sent_ref, rows_ref):
    rows, second_extent, third_extent = core_ref.shape
    second = second_ref[0, 0]
    third = third_ref[0, 0]
    term = pl.program_id(0)

    def one_row(row, carry):
        inner = lax.dot_general(
            core_ref[row],
            third,
            (((1,), (1,)), ((), ())),
            preferred_element_type=jnp.float32,
        ).astype(jnp.bfloat16)
        value = jnp.dot(second, inner, preferred_element_type=jnp.float32)
        for part in range(third_extent // LANES):
            rows_ref[part, pl.ds(row, second_extent, stride=rows), :] = value[
                :, part * LANES : (part + 1) * LANES
            ]
        return carry

    lax.fori_loop(0, rows, one_row, 0, unroll=UNROLL)
    for part in range(third_extent // LANES):
        sent_ref[:, term, :, part * LANES : (part + 1) * LANES] = (
            rows_ref[part].astype(jnp.bfloat16).reshape(*sent_ref.shape[:1], sent_ref.shape[2], LANES)
        )


def apply_first(first_ref, got_ref, sent_ref):
    states, _, first_extent, _ = first_ref.shape
    devices, terms, held, third_extent = got_ref.shape
    owners = devices // states
    rows = first_extent // owners

    def piece(source, term, column):
        value = got_ref[
            source * owners : (source + 1) * owners, term, column * rows : (column + 1) * rows
        ]
        return (
            value.astype(jnp.float32).reshape(first_extent, third_extent).astype(jnp.bfloat16)
        )

    for column in range(held // rows):
        for state in range(states):
            total = jnp.zeros((first_extent, third_extent), jnp.float32)
            for source, term in ((state, 0), (state, 1), (1 - state, 2)):
                total += jnp.dot(
                    first_ref[source, term],
                    piece(source, term, column),
                    preferred_element_type=jnp.float32,
                )
            sent_ref[
                state * owners : (state + 1) * owners, column * rows : (column + 1) * rows
            ] = total.reshape(owners, rows, third_extent).astype(jnp.bfloat16)


def relax(got_ref, core_ref, relaxed_ref, rows_ref):
    row = pl.program_id(0)
    rows = pl.num_programs(0)

    @pl.when(row == 0)
    def _():
        for part in range(rows_ref.shape[0]):
            rows_ref[part] = (
                got_ref[:, :, part * LANES : (part + 1) * LANES]
                .astype(jnp.float32)
                .reshape(rows_ref.shape[1:])
            )

    for part in range(rows_ref.shape[0]):
        lanes = slice(part * LANES, (part + 1) * LANES)
        applied = rows_ref[part, pl.ds(row, core_ref.shape[1], stride=rows), :]
        relaxed_ref[0, :, lanes] = core_ref[row, :, lanes].astype(jnp.float32) - 0.5 * applied


def in_vmem(value):
    return pltpu.with_memory_space_constraint(value, pltpu.VMEM)


def in_hbm(value):
    return pltpu.with_memory_space_constraint(value, pltpu.HBM)


def shards(core, op_one, op_two, op_three):
    own_core = core[0]
    rows, second_extent, third_extent = own_core.shape
    states, terms, first_extent, _ = op_one.shape
    devices = states * (first_extent // rows)
    held = second_extent // devices * rows
    state_index = lax.axis_index("state").astype(jnp.int32).reshape(1)
    whole = pl.BlockSpec(memory_space=pltpu.VMEM)

    sent = pl.pallas_call(
        prepare,
        grid_spec=pltpu.PrefetchScalarGridSpec(
            num_scalar_prefetch=1,
            grid=(terms,),
            in_specs=[
                pl.BlockSpec((rows, second_extent, third_extent), lambda term, state: (0, 0, 0)),
                pl.BlockSpec(
                    (1, 1, second_extent, second_extent), lambda term, state: (state[0], term, 0, 0)
                ),
                pl.BlockSpec(
                    (1, 1, third_extent, third_extent), lambda term, state: (state[0], term, 0, 0)
                ),
            ],
            out_specs=whole,
            scratch_shapes=[pltpu.VMEM((third_extent // LANES, rows * second_extent, LANES), jnp.float32)],
        ),
        out_shape=pltpu.VMEM((devices, terms, held, third_extent), jnp.bfloat16),
        compiler_params=pltpu.CompilerParams(vmem_limit_bytes=32 << 20),
        name="prepare",
    )(state_index, in_hbm(own_core), in_hbm(op_two), in_hbm(op_three))
    got = lax.all_to_all(sent, EVERY, split_axis=0, concat_axis=0, tiled=True)
    applied = pl.pallas_call(
        apply_first,
        in_specs=[whole, whole],
        out_specs=whole,
        out_shape=pltpu.VMEM((devices, held, third_extent), jnp.bfloat16),
        compiler_params=pltpu.CompilerParams(vmem_limit_bytes=16 << 20),
        name="apply_first",
    )(in_vmem(op_one), in_vmem(got))
    returned = lax.all_to_all(applied, EVERY, split_axis=0, concat_axis=0, tiled=True)
    relaxed = pl.pallas_call(
        relax,
        grid=(rows,),
        in_specs=[whole, whole],
        out_specs=pl.BlockSpec((1, second_extent, third_extent), lambda row: (row, 0, 0)),
        scratch_shapes=[pltpu.VMEM((third_extent // LANES, rows * second_extent, LANES), jnp.float32)],
        out_shape=jax.ShapeDtypeStruct(own_core.shape, jnp.float32),
        compiler_params=pltpu.CompilerParams(vmem_limit_bytes=24 << 20),
        name="relax",
    )(in_vmem(returned), in_vmem(own_core))
    return relaxed[None]


def solution(mesh):
    placed = (P("state", "mode", None, None), P(), P(), P())
    return jax.shard_map(
        shards,
        mesh=mesh,
        in_specs=placed,
        out_specs=P("state", "mode", None, None),
        check_vma=False,
    )
```

```python
import jax
import jax.numpy as jnp
from jax import lax
from jax.experimental import pallas as pl
from jax.experimental.pallas import tpu as pltpu
from jax.sharding import PartitionSpec as P

EVERY = ("state", "mode")
LANES = 128
PITCH = 12
GROUP = 4
BLOCKS = 8


def prepare(state_ref, core_ref, second_ref, third_ref, sent_ref, inner_ref, rows_ref):
    rows, second_extent, third_extent = core_ref.shape
    devices, _, parts, held, _ = sent_ref.shape
    second = second_ref[0, 0]
    third = third_ref[0, 0]
    term = pl.program_id(0)
    for row in range(rows):
        inner_ref[:, row * third_extent : (row + 1) * third_extent] = lax.dot_general(
            core_ref[row],
            third,
            (((1,), (1,)), ((), ())),
            preferred_element_type=jnp.float32,
        ).astype(jnp.bfloat16)
    for first in range(0, rows, GROUP):
        value = jnp.dot(
            second,
            inner_ref[:, first * third_extent : (first + GROUP) * third_extent],
            preferred_element_type=jnp.float32,
        )
        for row in range(GROUP):
            for part in range(parts):
                lane = row * third_extent + part * LANES
                rows_ref[part, pl.ds(first + row, second_extent, stride=PITCH), :] = value[
                    :, lane : lane + LANES
                ]
    for part in range(parts):
        turned = jnp.stack(
            [rows_ref[part, at * PITCH : at * PITCH + rows] for at in range(second_extent)]
        )
        sent_ref[:, term, part] = turned.astype(jnp.bfloat16).reshape(devices, held, LANES)


def apply_first(first_ref, got_ref, sent_ref):
    states, _, first_extent, _ = first_ref.shape
    devices, _, parts, held, _ = got_ref.shape
    owners = devices // states
    rows = first_extent // owners

    def piece(source, term, column):
        values = [
            got_ref[
                source * owners : (source + 1) * owners,
                term,
                part,
                column * rows : (column + 1) * rows,
            ]
            .astype(jnp.float32)
            .reshape(first_extent, LANES)
            .astype(jnp.bfloat16)
            for part in range(parts)
        ]
        return jnp.concatenate(values, axis=1)

    for column in range(held // rows):
        for state in range(states):
            total = jnp.zeros((first_extent, parts * LANES), jnp.float32)
            for source, term in ((state, 0), (state, 1), (1 - state, 2)):
                total += jnp.dot(
                    first_ref[source, term],
                    piece(source, term, column),
                    preferred_element_type=jnp.float32,
                )
            for part in range(parts):
                sent_ref[
                    state * owners : (state + 1) * owners,
                    part,
                    column * rows : (column + 1) * rows,
                ] = (
                    total[:, part * LANES : (part + 1) * LANES]
                    .reshape(owners, rows, LANES)
                    .astype(jnp.bfloat16)
                )


def relax(got_ref, core_ref, relaxed_ref, rows_ref):
    block = pl.program_id(0)
    rows, columns, _ = relaxed_ref.shape
    _, parts, held, _ = got_ref.shape
    owners = columns * rows // held
    for part in range(parts):
        value = got_ref[pl.ds(block * owners, owners), part].astype(jnp.float32)
        value = value.reshape(columns, rows, LANES)
        for column in range(columns):
            rows_ref[part, column * PITCH : column * PITCH + rows] = value[column]
    for row in range(rows):
        for part in range(parts):
            lanes = slice(part * LANES, (part + 1) * LANES)
            applied = rows_ref[part, pl.ds(row, columns, stride=PITCH), :]
            kept = core_ref[row, pl.ds(block * columns, columns), lanes]
            relaxed_ref[row, :, lanes] = kept.astype(jnp.float32) - 0.5 * applied


def in_vmem(value):
    return pltpu.with_memory_space_constraint(value, pltpu.VMEM)


def in_hbm(value):
    return pltpu.with_memory_space_constraint(value, pltpu.HBM)


def shards(core, op_one, op_two, op_three):
    own_core = core[0]
    rows, second_extent, third_extent = own_core.shape
    states, terms, first_extent, _ = op_one.shape
    devices = states * (first_extent // rows)
    held = second_extent // devices * rows
    parts = third_extent // LANES
    columns = second_extent // BLOCKS
    state_index = lax.axis_index("state").astype(jnp.int32).reshape(1)
    whole = pl.BlockSpec(memory_space=pltpu.VMEM)

    sent = pl.pallas_call(
        prepare,
        grid_spec=pltpu.PrefetchScalarGridSpec(
            num_scalar_prefetch=1,
            grid=(terms,),
            in_specs=[
                pl.BlockSpec((rows, second_extent, third_extent), lambda term, state: (0, 0, 0)),
                pl.BlockSpec(
                    (1, 1, second_extent, second_extent), lambda term, state: (state[0], term, 0, 0)
                ),
                pl.BlockSpec(
                    (1, 1, third_extent, third_extent), lambda term, state: (state[0], term, 0, 0)
                ),
            ],
            out_specs=whole,
            scratch_shapes=[
                pltpu.VMEM((second_extent, rows * third_extent), jnp.bfloat16),
                pltpu.VMEM((parts, second_extent * PITCH, LANES), jnp.float32),
            ],
        ),
        out_shape=pltpu.VMEM((devices, terms, parts, held, LANES), jnp.bfloat16),
        compiler_params=pltpu.CompilerParams(vmem_limit_bytes=36 << 20),
        name="prepare",
    )(state_index, in_hbm(own_core), in_hbm(op_two), in_hbm(op_three))
    got = lax.all_to_all(sent, EVERY, split_axis=0, concat_axis=0, tiled=True)
    applied = pl.pallas_call(
        apply_first,
        in_specs=[whole, whole],
        out_specs=whole,
        out_shape=pltpu.VMEM((devices, parts, held, LANES), jnp.bfloat16),
        compiler_params=pltpu.CompilerParams(vmem_limit_bytes=16 << 20),
        name="apply_first",
    )(in_vmem(op_one), in_vmem(got))
    returned = lax.all_to_all(applied, EVERY, split_axis=0, concat_axis=0, tiled=True)
    relaxed = pl.pallas_call(
        relax,
        grid=(BLOCKS,),
        in_specs=[whole, whole],
        out_specs=pl.BlockSpec((rows, columns, third_extent), lambda block: (0, block, 0)),
        scratch_shapes=[pltpu.VMEM((parts, columns * PITCH, LANES), jnp.float32)],
        out_shape=jax.ShapeDtypeStruct(own_core.shape, jnp.float32),
        compiler_params=pltpu.CompilerParams(vmem_limit_bytes=24 << 20),
        name="relax",
    )(in_vmem(returned), in_vmem(own_core))
    return relaxed[None]


def solution(mesh):
    placed = (P("state", "mode", None, None), P(), P(), P())
    return jax.shard_map(
        shards,
        mesh=mesh,
        in_specs=placed,
        out_specs=P("state", "mode", None, None),
        check_vma=False,
    )
```

```python
import jax
import jax.numpy as jnp
from jax import lax
from jax.experimental import pallas as pl
from jax.experimental.pallas import tpu as pltpu
from jax.sharding import PartitionSpec as P

EVERY = ("state", "mode")
LANES = 128
PITCH = 12
GROUP = 2
BLOCKS = 2
SIDE = 4


def prepare(state_ref, core_ref, second_ref, third_ref, sent_ref, inner_ref, rows_ref):
    rows, second_extent, third_extent = core_ref.shape
    devices, _, parts, held, _ = sent_ref.shape
    second = second_ref[0, 0]
    third = third_ref[0, 0]
    term = pl.program_id(0)
    def stage(row):
        inner = lax.dot_general(
            core_ref[row],
            third,
            (((1,), (1,)), ((), ())),
            preferred_element_type=jnp.float32,
        ).astype(jnp.bfloat16)
        for part in range(parts):
            inner_ref[row, part] = inner[:, part * LANES : (part + 1) * LANES]

    for row in range(GROUP):
        stage(row)
    for first in range(0, rows, GROUP):
        for row in range(first + GROUP, min(first + 2 * GROUP, rows)):
            stage(row)
        inner = jnp.concatenate(
            [inner_ref[first + row, part] for row in range(GROUP) for part in range(parts)], axis=1
        )
        value = jnp.dot(second, inner, preferred_element_type=jnp.float32)
        for row in range(GROUP):
            for part in range(parts):
                lane = row * third_extent + part * LANES
                rows_ref[part, pl.ds(first + row, second_extent, stride=PITCH), :] = value[
                    :, lane : lane + LANES
                ]
    for part in range(parts):
        turned = jnp.stack(
            [rows_ref[part, at * PITCH : at * PITCH + rows] for at in range(second_extent)]
        )
        sent_ref[:, term, part] = turned.astype(jnp.bfloat16).reshape(devices, held, LANES)


def apply_first(first_ref, got_ref, sent_ref):
    states, _, first_extent, _ = first_ref.shape
    devices, _, parts, held, _ = got_ref.shape
    owners = devices // states
    rows = first_extent // owners

    def piece(source, term, column):
        values = [
            got_ref[
                source * owners : (source + 1) * owners,
                term,
                part,
                column * rows : (column + 1) * rows,
            ]
            .astype(jnp.float32)
            .reshape(first_extent, LANES)
            .astype(jnp.bfloat16)
            for part in range(parts)
        ]
        return jnp.concatenate(values, axis=1)

    for first in range(0, held // rows, SIDE):
        columns = range(first, first + SIDE)
        for state in range(states):
            total = jnp.zeros((first_extent, SIDE * parts * LANES), jnp.float32)
            for source, term in ((state, 0), (state, 1), (1 - state, 2)):
                total += jnp.dot(
                    first_ref[source, term],
                    jnp.concatenate([piece(source, term, column) for column in columns], axis=1),
                    preferred_element_type=jnp.float32,
                )
            for column in columns:
                for part in range(parts):
                    lane = ((column - first) * parts + part) * LANES
                    sent_ref[
                        state * owners : (state + 1) * owners,
                        part,
                        column * rows : (column + 1) * rows,
                    ] = (
                        total[:, lane : lane + LANES]
                        .reshape(owners, rows, LANES)
                        .astype(jnp.bfloat16)
                    )


def relax(got_ref, core_ref, relaxed_ref, rows_ref):
    block = pl.program_id(0)
    rows, columns, _ = relaxed_ref.shape
    _, parts, held, _ = got_ref.shape
    owners = columns * rows // held
    for part in range(parts):
        value = got_ref[pl.ds(block * owners, owners), part].astype(jnp.float32)
        value = value.reshape(columns, rows, LANES)
        for column in range(columns):
            rows_ref[part, column * PITCH : column * PITCH + rows] = value[column]
    for row in range(rows):
        for part in range(parts):
            lanes = slice(part * LANES, (part + 1) * LANES)
            applied = rows_ref[part, pl.ds(row, columns, stride=PITCH), :]
            kept = core_ref[row, pl.ds(block * columns, columns), lanes]
            relaxed_ref[row, :, lanes] = kept.astype(jnp.float32) - 0.5 * applied


def in_vmem(value):
    return pltpu.with_memory_space_constraint(value, pltpu.VMEM)


def in_hbm(value):
    return pltpu.with_memory_space_constraint(value, pltpu.HBM)


def shards(core, op_one, op_two, op_three):
    own_core = core[0]
    rows, second_extent, third_extent = own_core.shape
    states, terms, first_extent, _ = op_one.shape
    devices = states * (first_extent // rows)
    held = second_extent // devices * rows
    parts = third_extent // LANES
    columns = second_extent // BLOCKS
    state_index = lax.axis_index("state").astype(jnp.int32).reshape(1)
    whole = pl.BlockSpec(memory_space=pltpu.VMEM)

    sent = pl.pallas_call(
        prepare,
        grid_spec=pltpu.PrefetchScalarGridSpec(
            num_scalar_prefetch=1,
            grid=(terms,),
            in_specs=[
                pl.BlockSpec((rows, second_extent, third_extent), lambda term, state: (0, 0, 0)),
                pl.BlockSpec(
                    (1, 1, second_extent, second_extent), lambda term, state: (state[0], term, 0, 0)
                ),
                pl.BlockSpec(
                    (1, 1, third_extent, third_extent), lambda term, state: (state[0], term, 0, 0)
                ),
            ],
            out_specs=whole,
            scratch_shapes=[
                pltpu.VMEM((rows, parts, second_extent, LANES), jnp.bfloat16),
                pltpu.VMEM((parts, second_extent * PITCH, LANES), jnp.float32),
            ],
        ),
        out_shape=pltpu.VMEM((devices, terms, parts, held, LANES), jnp.bfloat16),
        compiler_params=pltpu.CompilerParams(vmem_limit_bytes=36 << 20),
        name="prepare",
    )(state_index, in_hbm(own_core), in_hbm(op_two), in_hbm(op_three))
    got = lax.all_to_all(sent, EVERY, split_axis=0, concat_axis=0, tiled=True)
    applied = pl.pallas_call(
        apply_first,
        in_specs=[whole, whole],
        out_specs=whole,
        out_shape=pltpu.VMEM((devices, parts, held, LANES), jnp.bfloat16),
        compiler_params=pltpu.CompilerParams(vmem_limit_bytes=16 << 20),
        name="apply_first",
    )(in_vmem(op_one), in_vmem(got))
    returned = lax.all_to_all(applied, EVERY, split_axis=0, concat_axis=0, tiled=True)
    relaxed = pl.pallas_call(
        relax,
        grid=(BLOCKS,),
        in_specs=[whole, whole],
        out_specs=pl.BlockSpec((rows, columns, third_extent), lambda block: (0, block, 0)),
        scratch_shapes=[pltpu.VMEM((parts, columns * PITCH, LANES), jnp.float32)],
        out_shape=jax.ShapeDtypeStruct(own_core.shape, jnp.float32),
        compiler_params=pltpu.CompilerParams(vmem_limit_bytes=24 << 20),
        name="relax",
    )(in_vmem(returned), in_vmem(own_core))
    return relaxed[None]


def solution(mesh):
    placed = (P("state", "mode", None, None), P(), P(), P())
    return jax.shard_map(
        shards,
        mesh=mesh,
        in_specs=placed,
        out_specs=P("state", "mode", None, None),
        check_vma=False,
    )
```

```python
import jax
import jax.numpy as jnp
from jax import lax
from jax.experimental import pallas as pl
from jax.experimental.pallas import tpu as pltpu
from jax.sharding import PartitionSpec as P

EVERY = ("state", "mode")
LANES = 128
HALF = 4
PITCH = 12
GROUP = 2
BLOCKS = 4
SIDE = 4


def prepare(
    state_ref,
    core_hbm,
    second_hbm,
    third_hbm,
    sent_ref,
    core_ref,
    second_ref,
    third_ref,
    inner_ref,
    rows_ref,
    core_sems,
    second_sems,
    third_sems,
):
    rows, second_extent, third_extent = core_ref.shape
    devices, terms, parts, held, _ = sent_ref.shape
    state = state_ref[0]
    groups = range(0, rows, GROUP)
    cores = {
        first: pltpu.make_async_copy(
            core_hbm.at[pl.ds(first, HALF)],
            core_ref.at[pl.ds(first, HALF)],
            core_sems.at[first // HALF],
        )
        for first in range(0, rows, HALF)
    }
    seconds = [
        pltpu.make_async_copy(second_hbm.at[state, term], second_ref.at[term], second_sems.at[term])
        for term in range(terms)
    ]
    thirds = [
        pltpu.make_async_copy(third_hbm.at[state, term], third_ref.at[term], third_sems.at[term])
        for term in range(terms)
    ]

    def stage(term, first):
        for row in range(first, first + GROUP):
            inner = lax.dot_general(
                core_ref[row],
                third_ref[term],
                (((1,), (1,)), ((), ())),
                preferred_element_type=jnp.float32,
            ).astype(jnp.bfloat16)
            for part in range(parts):
                inner_ref[row, part] = inner[:, part * LANES : (part + 1) * LANES]

    def spread(term, first):
        inner = jnp.concatenate(
            [inner_ref[first + row, part] for row in range(GROUP) for part in range(parts)], axis=1
        )
        value = jnp.dot(second_ref[term], inner, preferred_element_type=jnp.float32)
        for row in range(GROUP):
            for part in range(parts):
                lane = row * third_extent + part * LANES
                rows_ref[term % 2, part, pl.ds(first + row, second_extent, stride=PITCH), :] = value[
                    :, lane : lane + LANES
                ]

    def send(term, first, count):
        owners = count * rows // held
        low = first * rows // held
        for part in range(parts):
            turned = jnp.stack(
                [
                    rows_ref[term % 2, part, at * PITCH : at * PITCH + rows]
                    for at in range(first, first + count)
                ]
            )
            sent_ref[low : low + owners, term, part] = turned.astype(jnp.bfloat16).reshape(
                owners, held, LANES
            )

    thirds[0].start()
    seconds[0].start()
    for first in range(0, rows, HALF):
        cores[first].start()
    for term in range(1, terms):
        thirds[term].start()
        seconds[term].start()
    thirds[0].wait()
    seconds[0].wait()
    for half in range(0, rows, HALF):
        cores[half].wait()
        stage(0, half)
        for first in range(half, half + HALF, GROUP):
            if first + GROUP < half + HALF:
                stage(0, first + GROUP)
            spread(0, first)
    for term in range(1, terms):
        thirds[term].wait()
        seconds[term].wait()
    share = second_extent // len(groups)
    for term in range(1, terms):
        stage(term, 0)
        for turn, first in enumerate(groups):
            if first + GROUP < rows:
                stage(term, first + GROUP)
            spread(term, first)
            send(term - 1, turn * share, share)
    send(terms - 1, 0, second_extent)


def apply_first(first_ref, got_ref, sent_ref):
    states, _, first_extent, _ = first_ref.shape
    devices, _, parts, held, _ = got_ref.shape
    owners = devices // states
    rows = first_extent // owners

    def piece(source, term, column):
        values = [
            got_ref[
                source * owners : (source + 1) * owners,
                term,
                part,
                column * rows : (column + 1) * rows,
            ]
            .astype(jnp.float32)
            .reshape(first_extent, LANES)
            .astype(jnp.bfloat16)
            for part in range(parts)
        ]
        return jnp.concatenate(values, axis=1)

    for first in range(0, held // rows, SIDE):
        columns = range(first, first + SIDE)
        for state in range(states):
            total = jnp.zeros((first_extent, SIDE * parts * LANES), jnp.float32)
            for source, term in ((state, 0), (state, 1), (1 - state, 2)):
                total += jnp.dot(
                    first_ref[source, term],
                    jnp.concatenate([piece(source, term, column) for column in columns], axis=1),
                    preferred_element_type=jnp.float32,
                )
            for column in columns:
                for part in range(parts):
                    lane = ((column - first) * parts + part) * LANES
                    sent_ref[
                        state * owners : (state + 1) * owners,
                        part,
                        column * rows : (column + 1) * rows,
                    ] = (
                        total[:, lane : lane + LANES]
                        .reshape(owners, rows, LANES)
                        .astype(jnp.bfloat16)
                    )


def relax(got_ref, core_ref, relaxed_hbm, rows_ref, out_ref, sems):
    rows, second_extent, _ = core_ref.shape
    _, parts, held, _ = got_ref.shape
    columns = second_extent // BLOCKS
    owners = columns * rows // held
    copies = []
    for block in range(BLOCKS):
        low = block * columns
        for part in range(parts):
            value = got_ref[block * owners : (block + 1) * owners, part].astype(jnp.float32)
            value = value.reshape(columns, rows, LANES)
            for column in range(columns):
                at = (low + column) * PITCH
                rows_ref[part, at : at + rows] = value[column]
        for row in range(rows):
            for part in range(parts):
                lanes = slice(part * LANES, (part + 1) * LANES)
                applied = rows_ref[part, pl.ds(low * PITCH + row, columns, stride=PITCH), :]
                kept = core_ref[row, low : low + columns, lanes]
                out_ref[row, low : low + columns, lanes] = (
                    kept.astype(jnp.float32) - 0.5 * applied
                )
        copies.append(
            pltpu.make_async_copy(
                out_ref.at[:, pl.ds(low, columns)],
                relaxed_hbm.at[:, pl.ds(low, columns)],
                sems.at[block],
            )
        )
        copies[-1].start()
    for copy in copies:
        copy.wait()


def in_vmem(value):
    return pltpu.with_memory_space_constraint(value, pltpu.VMEM)


def in_hbm(value):
    return pltpu.with_memory_space_constraint(value, pltpu.HBM)


def shards(core, op_one, op_two, op_three):
    own_core = core[0]
    rows, second_extent, third_extent = own_core.shape
    states, terms, first_extent, _ = op_one.shape
    devices = states * (first_extent // rows)
    held = second_extent // devices * rows
    parts = third_extent // LANES
    state_index = lax.axis_index("state").astype(jnp.int32).reshape(1)
    whole = pl.BlockSpec(memory_space=pltpu.VMEM)

    sent = pl.pallas_call(
        prepare,
        in_specs=[pl.BlockSpec(memory_space=pltpu.SMEM)]
        + [pl.BlockSpec(memory_space=pltpu.HBM)] * 3,
        out_specs=whole,
        scratch_shapes=[
            pltpu.VMEM((rows, second_extent, third_extent), jnp.bfloat16),
            pltpu.VMEM((terms, second_extent, second_extent), jnp.bfloat16),
            pltpu.VMEM((terms, third_extent, third_extent), jnp.bfloat16),
            pltpu.VMEM((rows, parts, second_extent, LANES), jnp.bfloat16),
            pltpu.VMEM((2, parts, second_extent * PITCH, LANES), jnp.float32),
            pltpu.SemaphoreType.DMA((rows // HALF,)),
            pltpu.SemaphoreType.DMA((terms,)),
            pltpu.SemaphoreType.DMA((terms,)),
        ],
        out_shape=pltpu.VMEM((devices, terms, parts, held, LANES), jnp.bfloat16),
        compiler_params=pltpu.CompilerParams(vmem_limit_bytes=36 << 20),
        name="prepare",
    )(state_index, in_hbm(own_core), in_hbm(op_two), in_hbm(op_three))
    got = lax.all_to_all(sent, EVERY, split_axis=0, concat_axis=0, tiled=True)
    applied = pl.pallas_call(
        apply_first,
        in_specs=[whole, whole],
        out_specs=whole,
        out_shape=pltpu.VMEM((devices, parts, held, LANES), jnp.bfloat16),
        compiler_params=pltpu.CompilerParams(vmem_limit_bytes=16 << 20),
        name="apply_first",
    )(in_vmem(op_one), in_vmem(got))
    returned = lax.all_to_all(applied, EVERY, split_axis=0, concat_axis=0, tiled=True)
    relaxed = pl.pallas_call(
        relax,
        in_specs=[whole, whole],
        out_specs=pl.BlockSpec(memory_space=pltpu.HBM),
        scratch_shapes=[
            pltpu.VMEM((parts, second_extent * PITCH, LANES), jnp.float32),
            pltpu.VMEM(own_core.shape, jnp.float32),
            pltpu.SemaphoreType.DMA((BLOCKS,)),
        ],
        out_shape=jax.ShapeDtypeStruct(own_core.shape, jnp.float32),
        compiler_params=pltpu.CompilerParams(vmem_limit_bytes=24 << 20),
        name="relax",
    )(in_vmem(returned), in_vmem(own_core))
    return relaxed[None]


def solution(mesh):
    placed = (P("state", "mode", None, None), P(), P(), P())
    return jax.shard_map(
        shards,
        mesh=mesh,
        in_specs=placed,
        out_specs=P("state", "mode", None, None),
        check_vma=False,
    )
```
